32 devices in a mesh: slab: 8 (over z, x), tile: 4 (over y, core).
Axes of the slice: x: 2, y: 2, z: 4, core: 2. Of those that a mesh axis runs over, the one named last changes fastest.
Arguments:
- fixed_planes: float32 [128, 512, 128], P(('slab', 'tile')), may hold values from -6 to 6
- moving_planes: float32 [2, 128, 512, 128], P(None, ('slab', 'tile')), may hold values from -6 to 6
- pair_dest: int32 [2, 128], P(None, ('slab', 'tile')), may hold values from 0 to 7, as said below
- pair_slot: int32 [2, 128], P(None, ('slab', 'tile')), may hold values from 0 to 3, as said below
- plane_shift: int32 [2, 2, 128], P(None, None, ('slab', 'tile')), may hold values from -24 to 24
- live_count: int32 [32], P(('slab', 'tile')), may hold values from 1 to 4, 74 in all
- piece_block: int32 [2048], P(('slab', 'tile')), may hold values from 0 to 511, as said below
Outputs:
- peaks: float32 [2, 128], P(None, ('slab', 'tile'))
- blocks: float32 [512, 32, 128], P(('slab', 'tile'))
The draws below stay inside these ranges and needn't reach their ends.
Inputs may be any that keep to these rules, and one draw needn't show every extreme that they name: `pair_dest`: round 0 entries lie in 0 to 7 and round 1 entries in 0 to 3. With pair_slot, every fixed plane of every device is targeted by exactly one moving plane in each round. In round 0 no device targets more than 2 planes of any one device, in round 1 no more than 2; in every round every device targets exactly that many planes of some device. `pair_slot`: drawn together with pair_dest. `live_count`: the counts sum to 74 and some device has 4. `piece_block`: block b is owned by device b // 16 along slab+tile. At most 2 pieces of one device go to blocks of one owner, and the first 2 pieces of every device go to blocks of one owner.
All inputs are finite; a program needn't handle non-finite values.
Results may differ from the reference program's by a relative error of at most 0.0003.
Values sent between devices are 32-bit elements; how exact they have to be, the bound alone decides.
No kernel may reach another device: no remote copies, remote signals or barrier semaphores. Data moves between devices by JAX's collectives and lax.ppermute only.
A program may use at most 128 MiB of HBM per device.

```python
import math
import jax
import jax.numpy as jnp
import numpy as np
from jax import lax

H = 512
W = 128
STRIPS = 4
PIECES = 16
OWNED = 16
PLANES = 128
BLOCKS = 512
CAP_SLAB = 2
CAP_TILE = 2
ROUTE_CAP = 2
N_SLAB = 8
N_TILE = 4
DEVICES = 32


def group_matching(subkey, group_size, capacity):
    subkeys = jax.random.split(subkey, 7)
    full_bin = jax.random.randint(subkeys[0], (), 0, group_size)
    spread = jax.random.permutation(subkeys[1], (group_size - 1) * capacity)[:STRIPS - capacity]
    other_bins = spread // capacity
    other_bins = other_bins + (other_bins >= full_bin).astype(jnp.int32)
    bin_ids = lax.iota(jnp.int32, group_size)
    counts = capacity * (bin_ids == full_bin).astype(jnp.int32) + jnp.sum((other_bins[:, None] == bin_ids[None, :]).astype(jnp.int32), 0)
    offsets = jnp.cumsum(counts) - counts
    position = lax.iota(jnp.int32, STRIPS)
    inside = (position[:, None] >= offsets[None, :]) & (position[:, None] < (offsets + counts)[None, :])
    bin_of = jnp.sum(inside.astype(jnp.int32) * bin_ids[None, :], 1)
    row_order = jax.random.permutation(subkeys[2], group_size)
    column_order = jax.random.permutation(subkeys[3], group_size)
    relabel = jax.random.permutation(subkeys[4], group_size)
    orders = jax.vmap(lambda inner: jax.random.permutation(inner, STRIPS))(jax.random.split(subkeys[5], group_size))
    landings = jax.vmap(lambda inner: jax.random.permutation(inner, STRIPS))(jax.random.split(subkeys[6], group_size))
    bins_taken = bin_of[orders]
    target = relabel[(row_order[:, None] + column_order[bins_taken]) % group_size]
    landing = landings[target, orders]
    return (target.astype(jnp.int32), landing.astype(jnp.int32))


def matching(key):
    base = jax.random.fold_in(key, 4242)
    along_slab = jax.vmap(lambda inner: group_matching(inner, N_SLAB, CAP_SLAB))(jax.random.split(jax.random.fold_in(base, 1), N_TILE))
    along_tile = jax.vmap(lambda inner: group_matching(inner, N_TILE, CAP_TILE))(jax.random.split(jax.random.fold_in(base, 2), N_SLAB))
    first_target = jnp.transpose(along_slab[0], (1, 0, 2)).reshape(-1)
    first_landing = jnp.transpose(along_slab[1], (1, 0, 2)).reshape(-1)
    second_target = along_tile[0].reshape(-1)
    second_landing = along_tile[1].reshape(-1)
    return (jnp.stack([first_target, second_target]), jnp.stack([first_landing, second_landing]))


def draw_pair_dest(key, part):
    return matching(key)[0]


def draw_pair_slot(key, part):
    return matching(key)[1]


def owner_pieces(subkey):
    halves = jax.random.split(subkey, 2)
    slot_total = DEVICES * ROUTE_CAP
    order = jax.random.permutation(halves[0], slot_total)
    leader = order[0] // ROUTE_CAP
    ranks = lax.iota(jnp.int32, slot_total)
    score = jnp.where(order // ROUTE_CAP == leader, ranks - slot_total, ranks)
    arranged = order[jnp.argsort(score, stable=True)]
    picked = arranged[:STRIPS * PIECES]
    within = jax.random.randint(halves[1], (STRIPS * PIECES,), 0, OWNED)
    return (picked // ROUTE_CAP * OWNED + within).astype(jnp.int32)


def draw_piece_block(key, part):
    subkeys = jax.random.split(jax.random.fold_in(key, 9191), DEVICES)
    return jax.vmap(owner_pieces)(subkeys).reshape(-1)


def plant(values, stream_key, least, top_value):
    shape = values.shape
    place = [jax.random.randint(jax.random.fold_in(stream_key, axis), (), 0, shape[axis]) for axis in range(len(shape))]
    values = values.at[tuple(place)].set(least)
    longest = shape.index(max(shape))
    place[longest] = (place[longest] + 1) % shape[longest]
    return values.at[tuple(place)].set(top_value)


def steps_of(rng, shape, cuts, smallest, top_value):
    factor_of, own = 1.0, jax.random.fold_in(rng, 6)
    for axis_at, parts in cuts:
        heights = jnp.exp(jax.random.uniform(jax.random.fold_in(own, axis_at), (parts,), jnp.float32, smallest / len(cuts), top_value / len(cuts)))
        factor_of = factor_of * jnp.repeat(heights, shape[axis_at] // parts).reshape([-1 if axis == axis_at else 1 for axis in range(len(shape))])
    return factor_of


def length_profile(amount, total, most, slope):
    loads = [(1 << 20) // math.isqrt(grade ** slope) + 1 for grade in range(2, amount + 1)]
    surplus, holding = total - most - (amount - 1), [1] * (amount - 1)
    while surplus > 0:
        movable = [i for i in range(amount - 1) if holding[i] < most]
        mass, left = sum([loads[i] for i in movable]), surplus
        for i in movable:
            extra = min(most - holding[i], max(1, left * loads[i] // mass), surplus)
            holding[i] = holding[i] + extra
            surplus = surplus - extra
    return np.array([most] + holding)


def ragged_sizes(key, amount, total, reach, skew):
    if amount == 2:
        one = jax.random.randint(key, (), max(1, total - reach), min(reach, total - 1) + 1)
        return jnp.stack([one, total - one])
    lengths = jnp.asarray(length_profile(amount, total, reach, skew), jnp.int32)
    couples = (amount - 1) // 2
    source_of, receiver = lengths[1:1 + 2 * couples:2], lengths[2:2 + 2 * couples:2]
    margin = jnp.minimum(source_of - 1, reach - receiver)
    passed = jax.random.randint(jax.random.fold_in(key, 1), (couples,), 0, 1 << 20) % (margin + 1)
    lengths = lengths.at[1:1 + 2 * couples:2].set(source_of - passed).at[2:2 + 2 * couples:2].set(receiver + passed)
    return lengths[jax.random.permutation(jax.random.fold_in(key, 2), amount)]


def gaussian(stream_key, shape, deviation, limit, shards=(), kind=jnp.bfloat16):
    result = deviation * jax.random.normal(stream_key, shape, jnp.float32)
    if shards:
        result = result * steps_of(stream_key, shape, shards, -0.22, 0.18)
    return jnp.clip(result, -limit, limit).astype(kind)


def setup_inputs(seed: int = 0) -> dict:
    seeds = jax.random.split(jax.random.key(seed), 8)
    fixed_planes = gaussian(seeds[0], (PLANES, H, W), 1.0, 6.0, ((0, 32),), jnp.float32)
    moving_planes = gaussian(seeds[1], (2, PLANES, H, W), 1.0, 6.0, ((1, 32),), jnp.float32)
    pair_dest = draw_pair_dest(jax.random.fold_in(seeds[7], 71), 0)
    pair_slot = draw_pair_slot(jax.random.fold_in(seeds[7], 71), 0)
    plane_shift = plant(jax.random.randint(seeds[4], (2, 2, PLANES), -24, 25), jax.random.fold_in(seeds[4], 1), -24, 24).astype(jnp.int32)
    live_count = ragged_sizes(seeds[5], DEVICES, DEVICES * STRIPS * 7 // 12, STRIPS, 2).astype(jnp.int32)
    piece_block = draw_piece_block(jax.random.fold_in(seeds[7], 71), 0)
    return {"fixed_planes": fixed_planes, "moving_planes": moving_planes, "pair_dest": pair_dest, "pair_slot": pair_slot, "plane_shift": plane_shift, "live_count": live_count, "piece_block": piece_block}


FLOOR = 0.25
CENTER = 4.0

def correlate(spectrum, partner):
    moving_spectrum = jnp.fft.fft2(partner, norm='ortho')
    cross = spectrum * jnp.conj(moving_spectrum)
    magnitude = jnp.sqrt(jnp.real(cross) ** 2 + jnp.imag(cross) ** 2 + FLOOR ** 2)
    surface = jnp.real(jnp.fft.ifft2(cross / magnitude, norm='ortho'))
    return lax.optimization_barrier(jnp.max(surface, axis=(1, 2)))

def shift_planes(planes, downward, sideways):
    return jax.vmap(lambda plane, first_shift, second_shift: jnp.roll(plane, (first_shift, second_shift), axis=(0, 1)))(planes, downward, sideways)

def reference(fixed_planes, moving_planes, pair_dest, pair_slot, plane_shift, live_count, piece_block):
    plane_total = fixed_planes.shape[0]
    strip_index = jnp.arange(plane_total, dtype=jnp.int32)
    device = strip_index // STRIPS
    slab_place = device // N_TILE
    tile_place = device % N_TILE
    first_target = (pair_dest[0] * N_TILE + tile_place) * STRIPS + pair_slot[0]
    second_target = (slab_place * N_TILE + pair_dest[1]) * STRIPS + pair_slot[1]
    sources = [jnp.zeros((plane_total,), jnp.int32).at[target].set(strip_index) for target in (first_target, second_target)]

    def one_device(device_index):
        first_row = (device_index * STRIPS).astype(jnp.int32)
        fixed_part = lax.dynamic_slice_in_dim(fixed_planes, first_row, STRIPS, 0)
        spectrum = jnp.fft.fft2(fixed_part, norm='ortho')
        is_live = jnp.arange(STRIPS, dtype=jnp.int32) < live_count[device_index]
        weighted_sum = fixed_part
        weight_total = jnp.ones((STRIPS,), fixed_part.dtype)
        peak_list = []
        for round_index in range(2):
            chosen = lax.dynamic_slice_in_dim(sources[round_index], first_row, STRIPS, 0)
            partner = moving_planes[round_index][chosen]
            peak_value = correlate(spectrum, partner)
            weight = jax.nn.sigmoid(peak_value - CENTER)
            shifts = lax.dynamic_slice_in_dim(plane_shift[round_index], first_row, STRIPS, 1)
            weighted_sum = weighted_sum + weight[:, None, None] * shift_planes(partner, shifts[0], shifts[1])
            weight_total = weight_total + weight
            peak_list.append(jnp.where(is_live, peak_value, 0.0))
        return (jnp.stack(peak_list), weighted_sum / weight_total[:, None, None])
    peak_rows, merged = lax.map(one_device, jnp.arange(plane_total // STRIPS, dtype=jnp.int32))
    peaks = jnp.transpose(peak_rows, (1, 0, 2)).reshape(2, plane_total)
    band_rows = H // PIECES
    pieces = merged.reshape(plane_total * PIECES, band_rows, W)
    piece_index = jnp.arange(plane_total * PIECES, dtype=jnp.int32)
    piece_live = piece_index // PIECES % STRIPS < jnp.repeat(live_count, STRIPS * PIECES)
    kept_pieces = jnp.where(piece_live[:, None, None], pieces, 0.0)
    blocks = jax.ops.segment_sum(kept_pieces, piece_block, num_segments=BLOCKS)
    return (peaks, blocks)
```

```python
import functools
import math

import jax
import jax.numpy as jnp
import numpy as np
from jax import lax
from jax.experimental import pallas as pl
from jax.experimental.pallas import tpu as pltpu
from jax.sharding import PartitionSpec as P

PIECES = 16
OWNED = 16
FLOOR = 0.25
CENTER = 4.0
PAD = 16
TILE = 8
F32, BF16, I32 = jnp.float32, jnp.bfloat16, jnp.int32
ANY = pl.BlockSpec(memory_space=pl.ANY)
SMEM = pl.BlockSpec(memory_space=pltpu.SMEM)


def halves(table):
    high = np.asarray(table, np.float32).astype(jnp.bfloat16)
    low = np.asarray(table - high.astype(np.float64), np.float32).astype(jnp.bfloat16)
    return high, low


@functools.lru_cache
def tables(height, breadth):
    half, quarter = height // 2, height // 4
    rows = np.arange(half)
    even = np.arange(quarter)[:, None] * 2 * rows[None, :] % height * (2 * math.pi / height)
    odd = (np.arange(quarter)[:, None] * 2 + 1) * rows[None, :] % height * (2 * math.pi / height)
    scale = 1 / math.sqrt(height)
    alternating = np.cos(math.pi * rows)
    even_sine = -np.sin(even)
    even_sine[0] = alternating
    ahead_even = np.concatenate([np.cos(even), even_sine], 0) * scale
    ahead_odd = np.concatenate([np.cos(odd), -np.sin(odd)], 0) * scale
    back_cosine = 2 * np.cos(even)
    back_cosine[0] = 1
    back_sine = 2 * np.sin(even)
    back_sine[0] = alternating
    back_even = np.concatenate([back_cosine, back_sine], 0).T * scale
    back_odd = np.concatenate([2 * np.cos(odd), 2 * np.sin(odd)], 0).T * scale
    index = np.arange(breadth)
    angle = index[:, None] * index[None, :] % breadth * (2 * math.pi / breadth)
    cosine, sine = np.cos(angle) / math.sqrt(breadth), np.sin(angle) / math.sqrt(breadth)
    across = np.block([[cosine, -sine], [sine, cosine]])
    pairs = [halves(t) for t in (ahead_even, ahead_odd, across, back_even, back_odd)]
    return [half_table for pair in pairs for half_table in pair]


def split(x):
    high = x.astype(BF16)
    return high, (x - high.astype(F32)).astype(BF16)


def dot(a, b):
    return jnp.dot(a, b, preferred_element_type=F32)


def table_times(high, low, x):
    x_high, x_low = split(x)
    breadth = x.shape[1]
    both = dot(high[...], jnp.concatenate([x_high, x_low], 1))
    return both[:, :breadth] + both[:, breadth:] + dot(low[...], x_high)


def times_table(x, high, low):
    x_high, x_low = split(x)
    return dot(x_high, high[...]) + (dot(x_low, high[...]) + dot(x_high, low[...]))


def rows_of(shape):
    return lax.broadcasted_iota(I32, shape, 0)


def forward(x, even, odd, across):
    height, breadth = x.shape
    half, quarter = height // 2, height // 4
    top, bottom = x[:half], x[half:]
    e = table_times(*even, top + bottom)
    o = table_times(*odd, top - bottom)
    first = rows_of((quarter, breadth)) == 0
    sine = e[quarter:]
    last = jnp.where(rows_of((PAD, breadth)) == 0, sine[:PAD], 0.0)
    mixed = jnp.concatenate(
        [
            jnp.concatenate([e[:quarter], jnp.where(first, 0.0, sine)], 1),
            jnp.concatenate([o[:quarter], o[quarter:]], 1),
            jnp.concatenate([last, jnp.zeros_like(last)], 1),
        ],
        0,
    )
    return times_table(mixed, *across)


def peak_of(fixed, moving, across, even, odd):
    breadth = fixed.shape[1] // 2
    half = fixed.shape[0] - PAD
    quarter = half // 2
    fr, fi = fixed[:, :breadth], fixed[:, breadth:]
    gr, gi = moving[:, :breadth], moving[:, breadth:]
    real = fr * gr + fi * gi
    minus = fr * gi - fi * gr
    factor = lax.rsqrt(real * real + minus * minus + FLOOR**2)
    v = times_table(jnp.concatenate([real * factor, minus * factor], 1), *across)
    vr, vn = v[:, :breadth], v[:, breadth:]
    first = rows_of((quarter, breadth)) == 0
    last = jnp.broadcast_to(vr[half : half + 1], (quarter, breadth))
    e = table_times(*even, jnp.concatenate([vr[:quarter], jnp.where(first, last, vn[:quarter])], 0))
    o = table_times(*odd, jnp.concatenate([vr[quarter:half], vn[quarter:half]], 0))
    highest = e + jnp.abs(o)
    return jnp.max(jnp.max(highest, axis=0, keepdims=True), axis=1, keepdims=True)


def weight_of(peak):
    return 1.0 / (1.0 + jnp.exp(-(peak - CENTER)))


def rolled(x, down, across):
    height, breadth = x.shape
    x = pltpu.roll(x, jnp.where(across < 0, across + breadth, across), 1)
    return pltpu.roll(x, jnp.where(down < 0, down + height, down), 0)


def spread_kernel(count, sizes, pieces_ref, dest_ref, slot_ref, live_ref, moving_ref, *rest):
    slab, tile, capacity = sizes
    outs, slots_ref = rest[:slab], rest[slab]
    held, labels, in_sem, out_sem, label_sem = rest[slab + 1 :]
    planes, height, breadth = held.shape
    run = height // slab
    here = lax.axis_index("slab")
    for s in range(planes):
        pltpu.make_async_copy(moving_ref.at[0, s], held.at[s], in_sem.at[s]).start()
    pieces = pieces_ref[0:1, :]
    size = pieces_ref.shape[1]
    row = jnp.broadcast_to(pieces, (size, size))
    i, j = rows_of((size, size)), lax.broadcasted_iota(I32, (size, size), 1)
    column = jnp.broadcast_to(
        jnp.sum(jnp.where(i == j, row, 0).astype(F32), axis=1, keepdims=True), (size, size)
    ).astype(I32)
    same = (lax.shift_right_arithmetic(row, 4) == lax.shift_right_arithmetic(column, 4)) & (i < j)
    rank = jnp.sum(same.astype(F32), axis=0, keepdims=True).astype(I32)
    place = lax.shift_right_arithmetic(pieces, 4) * capacity + rank
    slots_ref[...] = jnp.broadcast_to(place, slots_ref.shape)
    lane = lax.broadcasted_iota(I32, (1, size), 1)
    kept = lane < jnp.minimum(live_ref[0] * PIECES, count)
    within = jnp.where(kept, (pieces & (OWNED - 1)) + 1, 0).astype(F32)
    block = tile * capacity
    for p in range(slab):
        match = (jnp.broadcast_to(place, (block, size)) - p * block) == rows_of((block, size))
        label = jnp.sum(jnp.where(match, within, 0.0), axis=1, keepdims=True) - 1.0
        labels[p] = jnp.broadcast_to(label, (block, breadth))
    target = jnp.zeros((block, breadth), F32)
    for s in range(planes):
        value = (dest_ref[0, s] * planes + slot_ref[0, s]).astype(F32)
        target = jnp.where(rows_of((block, breadth)) == s, value, target)
    right = lax.broadcasted_iota(I32, (block, breadth), 1) >= breadth // 2
    for p in range(slab):
        labels[p] = jnp.where(right, target, labels[p])
    tags = [
        pltpu.make_async_copy(labels.at[here ^ k], outs[k].at[pl.ds(planes * run, block)], label_sem.at[k])
        for k in range(slab)
    ]
    for tag in tags:
        tag.start()
    copies = []
    for s in range(planes):
        pltpu.make_async_copy(moving_ref.at[0, s], held.at[s], in_sem.at[s]).wait()
        for k in range(slab):
            rows = pl.ds(pl.multiple_of((here ^ k) * run, run), run)
            copy = pltpu.make_async_copy(
                held.at[s, rows], outs[k].at[pl.ds(s * run, run)], out_sem.at[s, k]
            )
            copy.start()
            copies.append(copy)
    for copy in tags + copies:
        copy.wait()


def pair_kernel(sizes, dest_ref, slot_ref, moving_ref, *rest):
    tile, capacity = sizes
    outs = rest[:tile]
    held, labels, in_sem, out_sem, label_sem = rest[tile:]
    planes, height, breadth = held.shape
    here = lax.axis_index("tile")
    for s in range(planes):
        pltpu.make_async_copy(moving_ref.at[1, s], held.at[s], in_sem.at[s]).start()
    steps, ranks = [], []
    for s in range(planes):
        steps.append(dest_ref[1, s] ^ here)
        ranks.append(sum(((steps[u] == steps[s]).astype(I32) for u in range(s)), jnp.int32(0)))
    for k in range(tile):
        label = jnp.full((TILE, breadth), -1.0, F32)
        for s in range(planes):
            rank = jnp.where(steps[s] == k, ranks[s], TILE)
            label = jnp.where(rows_of((TILE, breadth)) == rank, slot_ref[1, s].astype(F32), label)
        labels[k] = label
    tags = [
        pltpu.make_async_copy(labels.at[k], outs[k].at[pl.ds(capacity * height, TILE)], label_sem.at[k])
        for k in range(tile)
    ]
    for tag in tags:
        tag.start()
    for s in range(planes):
        pltpu.make_async_copy(moving_ref.at[1, s], held.at[s], in_sem.at[s]).wait()
        for k in range(tile):

            @pl.when(steps[s] == k)
            def _(s=s, k=k):
                rows = pl.ds(pl.multiple_of(ranks[s] * height, height), height)
                pltpu.make_async_copy(held.at[s], outs[k].at[rows], out_sem.at[s]).start()

    for tag in tags:
        tag.wait()
    for s in range(planes):
        pltpu.make_async_copy(held.at[s], outs[0].at[pl.ds(0, height)], out_sem.at[s]).wait()


def route_kernel(sizes, *rest):
    slab, planes, run, block, breadth = sizes
    ins, outs = rest[:slab], rest[slab : 2 * slab]
    held, tags, in_sem, tag_sem, out_sem = rest[2 * slab :]
    here = lax.axis_index("slab")
    for k in range(slab):
        pltpu.make_async_copy(ins[k].at[pl.ds(planes * run, TILE)], tags.at[k], tag_sem.at[k]).start()
    for k in range(slab):
        pltpu.make_async_copy(ins[k].at[pl.ds(0, planes * run)], held.at[k], in_sem.at[k]).start()
    for k in range(slab):
        pltpu.make_async_copy(ins[k].at[pl.ds(planes * run, TILE)], tags.at[k], tag_sem.at[k]).wait()
        pltpu.make_async_copy(ins[k].at[pl.ds(0, planes * run)], held.at[k], in_sem.at[k]).wait()
        for s in range(planes):
            target = tags[k, s, breadth - 1].astype(I32)
            step = (target // planes) ^ here
            rows = pl.ds(pl.multiple_of((target % planes) * run, run), run)
            for m in range(slab):

                @pl.when(step == m)
                def _(k=k, s=s, m=m, rows=rows):
                    pltpu.make_async_copy(
                        held.at[k, pl.ds(s * run, run)], outs[m].at[rows], out_sem.at[k, s]
                    ).start()

    for k in range(slab):
        for s in range(planes):
            pltpu.make_async_copy(
                held.at[k, pl.ds(s * run, run)], outs[0].at[pl.ds(0, run)], out_sem.at[k, s]
            ).wait()


def label_kernel(sizes, *rest):
    slab, tile, capacity, breadth = sizes
    ins, outs = rest[:slab], rest[slab:]
    slab_here, tile_here = lax.axis_index("slab"), lax.axis_index("tile")
    lane = lax.broadcasted_iota(I32, (1, breadth), 1)
    for m in range(tile):
        first = (tile_here ^ m) * capacity
        for k in range(slab):
            line = ins[k][pl.ds(first + capacity - 1, 1), :]
            for r in reversed(range(capacity - 1)):
                line = jnp.where(lane < (r + 1) * (TILE), ins[k][pl.ds(first + r, 1), :], line)
            outs[m][pl.ds(slab_here ^ k, 1), :] = line


def spectrum_kernel(live_ref, plane_ref, *rest):
    tabs, out_ref = rest[:6], rest[6]

    @pl.when(pl.program_id(0) < live_ref[0])
    def _():
        out_ref[0] = forward(plane_ref[0], tabs[0:2], tabs[2:4], tabs[4:6])


def second_kernel(sizes, live_ref, shift_ref, plane_ref, fixed_ref, *rest):
    tile, capacity = sizes
    tabs, ins = rest[:10], rest[10 : 10 + tile]
    sum_ref, stat_ref = rest[11 + tile : 13 + tile]
    held, tags, anchor, sem, tag_sem = rest[13 + tile :]
    height, breadth = held.shape[1:]
    step = pl.program_id(0)

    def fetch(t, slot):
        for k in range(tile):

            @pl.when(anchor[t] // capacity == k)
            def _(k=k):
                rows = pl.ds(pl.multiple_of(anchor[t] % capacity * height, height), height)
                pltpu.make_async_copy(ins[k].at[rows], held.at[slot], sem.at[slot]).start()

    @pl.when(step == 0)
    def _():
        for k in range(tile):
            source = ins[k].at[pl.ds(capacity * height, TILE)]
            pltpu.make_async_copy(source, tags.at[k], tag_sem.at[k]).start()
        for k in range(tile):
            source = ins[k].at[pl.ds(capacity * height, TILE)]
            pltpu.make_async_copy(source, tags.at[k], tag_sem.at[k]).wait()
            for r in range(capacity):
                label = tags[k, r, 0].astype(I32)

                @pl.when(label >= 0)
                def _(k=k, r=r, label=label):
                    anchor[label] = k * capacity + r

        fetch(0, 0)

    @pl.when(step + 1 < live_ref[0])
    def _():
        fetch(step + 1, (step + 1) % 2)

    @pl.when(step < live_ref[0])
    def _():
        slot = step % 2
        pltpu.make_async_copy(ins[0].at[pl.ds(0, height)], held.at[slot], sem.at[slot]).wait()
        partner = held[slot]
        moving = forward(partner, tabs[0:2], tabs[2:4], tabs[4:6])
        peak = peak_of(fixed_ref[0], moving, tabs[4:6], tabs[6:8], tabs[8:10])
        weight = weight_of(peak)
        moved = rolled(partner, shift_ref[1, 0, step], shift_ref[1, 1, step])
        sum_ref[0] = plane_ref[0] + weight * moved
        line = rows_of((TILE, breadth))
        stat_ref[0] = jnp.where(line == 0, jnp.broadcast_to(weight, line.shape), peak)

    @pl.when(step >= live_ref[0])
    def _():
        stat_ref[0] = jnp.zeros((TILE, breadth), F32)


def first_kernel(slab, live_ref, shift_ref, slot_ref, sum_ref, stat_ref, fixed_ref, *rest):
    tabs, ins = rest[:10], rest[10 : 10 + slab]
    send_ref, peak_ref, plane, staged, sem = rest[10 + slab :]
    run, breadth = ins[0].shape
    height = plane.shape[0]
    band = height // PIECES
    step = pl.program_id(0)
    here = lax.axis_index("slab")

    @pl.when(step < live_ref[0])
    def _():
        for k in range(slab):
            plane[pl.ds(pl.multiple_of((here ^ k) * run, run), run), :] = ins[k][...]
        partner = plane[...]
        moving = forward(partner, tabs[0:2], tabs[2:4], tabs[4:6])
        peak = peak_of(fixed_ref[0], moving, tabs[4:6], tabs[6:8], tabs[8:10])
        weight = weight_of(peak)
        other = stat_ref[0][0:1, 0:1]
        moved = rolled(partner, shift_ref[0, 0, step], shift_ref[0, 1, step])
        staged[step] = (sum_ref[0] + weight * moved) / (1.0 + weight + other)
        line = rows_of((TILE, breadth))
        peak_ref[0] = jnp.where(line == 0, jnp.broadcast_to(peak, line.shape), stat_ref[0])
        for b in range(PIECES):
            slot = slot_ref[0, step * PIECES + b]
            pltpu.make_async_copy(
                staged.at[step, pl.ds(b * band, band)],
                send_ref.at[pl.ds(pl.multiple_of(slot * band, band), band)],
                sem.at[step],
            ).start()

    @pl.when(step >= live_ref[0])
    def _():
        peak_ref[0] = jnp.zeros((TILE, breadth), F32)

    @pl.when(step == pl.num_programs(0) - 1)
    def _():
        for t in range(staged.shape[0]):

            @pl.when(t < live_ref[0])
            def _(t=t):
                pltpu.make_async_copy(
                    staged.at[t], send_ref.at[pl.ds(0, height)], sem.at[t]
                ).wait()


def gather_kernel(sizes, data_ref, *rest):
    slab, tile, capacity, parts = sizes
    ins, out_ref = rest[:tile], rest[tile]
    held, tags, sem, tag_sem = rest[tile + 1 :]
    band = out_ref.shape[1]
    total = data_ref.shape[0] // parts
    tile_here = lax.axis_index("tile")
    for m in range(tile):
        pltpu.make_async_copy(ins[m], tags.at[m], tag_sem.at[m]).start()
    for c in range(parts):
        rows = pl.ds(c * total, total)
        pltpu.make_async_copy(data_ref.at[rows], held.at[rows], sem.at[c]).start()
    out_ref[...] = jnp.zeros_like(out_ref)
    for m in range(tile):
        pltpu.make_async_copy(ins[m], tags.at[m], tag_sem.at[m]).wait()
    per = slab // parts
    for c in range(parts):
        rows = pl.ds(c * total, total)
        pltpu.make_async_copy(data_ref.at[rows], held.at[rows], sem.at[c]).wait()

        def add(n, _, c=c):
            p = c * per + n // tile
            q = n % tile
            for r in range(capacity):
                label = tags[q ^ tile_here, p, r * TILE].astype(I32)
                start = ((p * tile + q) * capacity + r) * band

                @pl.when(label >= 0)
                def _(label=label, start=start):
                    out_ref[label] += held[pl.ds(pl.multiple_of(start, band), band), :]

            return 0

        lax.fori_loop(0, per * tile, add, 0)


def call(kernel, out_shape, **kwargs):
    cost = kwargs.pop("cost", (1_000_000, 4_000_000))
    return pl.pallas_call(
        kernel,
        out_shape=out_shape,
        cost_estimate=pl.CostEstimate(flops=cost[0], bytes_accessed=cost[1], transcendentals=0),
        **kwargs,
    )


def exchange(arrays, axis):
    size = len(arrays)
    got = [arrays[0]] + [None] * (size - 1)
    for k in reversed(range(1, size)):
        got[k] = lax.ppermute(arrays[k], axis, [(i, i ^ k) for i in range(size)])
    return got


def local(fixed_planes, moving_planes, pair_dest, pair_slot, plane_shift, live_count, piece_block):
    planes, height, breadth = fixed_planes.shape
    slab, tile = lax.axis_size("slab"), lax.axis_size("tile")
    devices = slab * tile
    count = piece_block.shape[0]
    run = height // slab
    band = height // PIECES
    tile_capacity = max(2, (planes + tile - 1) // tile)
    capacity = max(2, (count + devices - 1) // devices)
    block = tile * capacity
    spectrum_rows = height // 2 + PAD
    dma = pltpu.SemaphoreType.DMA
    shape = jax.ShapeDtypeStruct
    tabs = [jnp.asarray(t) for t in tables(height, breadth)]
    whole = [pl.BlockSpec(t.shape, lambda t, *_: (0, 0)) for t in tabs]

    piece_row = jnp.pad(piece_block.reshape(1, count), ((0, 0), (0, breadth - count)), constant_values=-1)
    spread = call(
        functools.partial(spread_kernel, count, (slab, tile, capacity)),
        [shape((planes * run + block, breadth), F32)] * slab + [shape((TILE, breadth), I32)],
        in_specs=[pl.BlockSpec(memory_space=pltpu.VMEM), SMEM, SMEM, SMEM, ANY],
        out_specs=[ANY] * slab + [pl.BlockSpec(memory_space=pltpu.VMEM)],
        scratch_shapes=[
            pltpu.VMEM((planes, height, breadth), F32),
            pltpu.VMEM((slab, block, breadth), F32),
            dma((planes,)),
            dma((planes, slab)),
            dma((slab,)),
        ],
        name="spread",
    )(piece_row, pair_dest, pair_slot, live_count, moving_planes)
    slots = spread[slab]
    runs = exchange(spread[:slab], "slab")

    paired = call(
        functools.partial(pair_kernel, (tile, tile_capacity)),
        [shape((tile_capacity * height + TILE, breadth), F32)] * tile,
        in_specs=[SMEM, SMEM, ANY],
        out_specs=[ANY] * tile,
        scratch_shapes=[
            pltpu.VMEM((planes, height, breadth), F32),
            pltpu.VMEM((tile, TILE, breadth), F32),
            dma((planes,)),
            dma((planes,)),
            dma((tile,)),
        ],
        name="pair",
    )(pair_dest, pair_slot, moving_planes)
    second_partners = exchange(paired, "tile")

    def plane_spec(rows, columns):
        return pl.BlockSpec((1, rows, columns), lambda t, *_: (t, 0, 0))

    spectrum = call(
        spectrum_kernel,
        shape((planes, spectrum_rows, 2 * breadth), F32),
        grid_spec=pltpu.PrefetchScalarGridSpec(
            num_scalar_prefetch=1,
            grid=(planes,),
            in_specs=[plane_spec(height, breadth)] + whole[:6],
            out_specs=plane_spec(spectrum_rows, 2 * breadth),
        ),
        cost=(10**9, 4 * 10**6),
        name="spectrum",
    )(live_count, fixed_planes, *tabs[:6])

    routed = call(
        functools.partial(route_kernel, (slab, planes, run, block, breadth)),
        [shape((planes * run, breadth), F32)] * slab,
        in_specs=[ANY] * slab,
        out_specs=[ANY] * slab,
        scratch_shapes=[
            pltpu.VMEM((slab, planes * run, breadth), F32),
            pltpu.SMEM((slab, TILE, breadth), F32),
            dma((slab,)),
            dma((slab,)),
            dma((slab, planes)),
        ],
        name="route",
    )(*runs)
    first_partners = exchange(routed, "slab")

    labels = call(
        functools.partial(label_kernel, (slab, tile, capacity, breadth)),
        [shape((slab, breadth), F32)] * tile,
        grid=(1,),
        in_specs=[pl.BlockSpec((block, breadth), lambda i: (planes * run // block, 0))] * slab,
        out_specs=[pl.BlockSpec((slab, breadth), lambda i: (0, 0))] * tile,
        name="label",
    )(*runs)
    band_labels = exchange(labels, "tile")

    summed, stats = call(
        functools.partial(second_kernel, (tile, tile_capacity)),
        [shape((planes, height, breadth), F32), shape((planes, TILE, breadth), F32)],
        grid_spec=pltpu.PrefetchScalarGridSpec(
            num_scalar_prefetch=2,
            grid=(planes,),
            in_specs=[plane_spec(height, breadth), plane_spec(spectrum_rows, 2 * breadth)]
            + whole
            + [ANY] * (tile + 1),
            out_specs=[plane_spec(height, breadth), plane_spec(TILE, breadth)],
            scratch_shapes=[
                pltpu.VMEM((2, height, breadth), F32),
                pltpu.SMEM((tile, TILE, breadth), F32),
                pltpu.SMEM((planes,), I32),
                dma((2,)),
                dma((tile,)),
            ],
        ),
        cost=(2 * 10**9, 6 * 10**6),
        name="second",
    )(live_count, plane_shift, fixed_planes, spectrum, *tabs, *second_partners, routed[0])

    send, tops = call(
        functools.partial(first_kernel, slab),
        [shape((devices * capacity * band, breadth), F32), shape((planes, TILE, breadth), F32)],
        grid_spec=pltpu.PrefetchScalarGridSpec(
            num_scalar_prefetch=3,
            grid=(planes,),
            in_specs=[
                plane_spec(height, breadth),
                plane_spec(TILE, breadth),
                plane_spec(spectrum_rows, 2 * breadth),
            ]
            + whole
            + [pl.BlockSpec((run, breadth), lambda t, *_: (t, 0))] * slab,
            out_specs=[ANY, plane_spec(TILE, breadth)],
            scratch_shapes=[
                pltpu.VMEM((height, breadth), F32),
                pltpu.VMEM((planes, height, breadth), F32),
                dma((planes,)),
            ],
        ),
        cost=(2 * 10**9, 6 * 10**6),
        name="first",
    )(live_count, plane_shift, slots, summed, stats, spectrum, *tabs, *first_partners)

    arrived = lax.all_to_all(
        send.reshape(devices, capacity * band, breadth), ("slab", "tile"), 0, 0, tiled=True
    )
    blocks = call(
        functools.partial(gather_kernel, (slab, tile, capacity, 4)),
        shape((OWNED, band, breadth), F32),
        in_specs=[ANY] * (tile + 1),
        out_specs=pl.BlockSpec(memory_space=pltpu.VMEM),
        scratch_shapes=[
            pltpu.VMEM((devices * capacity * band, breadth), F32),
            pltpu.SMEM((tile, slab, breadth), F32),
            dma((4,)),
            dma((tile,)),
        ],
        name="gather",
    )(arrived.reshape(devices * capacity * band, breadth), *band_labels)
    return (jnp.transpose(tops[:, :2, 0]), blocks)


def solution(mesh):
    placed = (
        P(("slab", "tile"), None, None),
        P(None, ("slab", "tile"), None, None),
        P(None, ("slab", "tile")),
        P(None, ("slab", "tile")),
        P(None, None, ("slab", "tile")),
        P(("slab", "tile")),
        P(("slab", "tile")),
    )
    return jax.shard_map(
        local,
        mesh=mesh,
        in_specs=placed,
        out_specs=(P(None, ("slab", "tile")), P(("slab", "tile"), None, None)),
        check_vma=False,
    )
```

```python
import functools
import math

import jax
import jax.numpy as jnp
import numpy as np
from jax import lax
from jax.experimental import pallas as pl
from jax.experimental.pallas import tpu as pltpu
from jax.sharding import PartitionSpec as P

PIECES = 16
OWNED = 16
FLOOR = 0.25
CENTER = 4.0
PAD = 16
TILE = 8
F32, BF16, I32 = jnp.float32, jnp.bfloat16, jnp.int32
VMEM = pl.BlockSpec(memory_space=pltpu.VMEM)
HBM = pl.BlockSpec(memory_space=pltpu.HBM)
SMEM = pl.BlockSpec(memory_space=pltpu.SMEM)


def halves(table):
    high = np.asarray(table, np.float32).astype(jnp.bfloat16)
    low = np.asarray(table - high.astype(np.float64), np.float32).astype(jnp.bfloat16)
    return high, low


@functools.lru_cache
def tables(height, breadth):
    half, quarter = height // 2, height // 4
    rows = np.arange(half)
    even = np.arange(quarter)[:, None] * 2 * rows[None, :] % height * (2 * math.pi / height)
    odd = (np.arange(quarter)[:, None] * 2 + 1) * rows[None, :] % height * (2 * math.pi / height)
    scale = 1 / math.sqrt(height)
    alternating = np.cos(math.pi * rows)
    even_sine = -np.sin(even)
    even_sine[0] = alternating
    ahead_even = np.concatenate([np.cos(even), even_sine], 0) * scale
    ahead_odd = np.concatenate([np.cos(odd), -np.sin(odd)], 0) * scale
    back_cosine = 2 * np.cos(even)
    back_cosine[0] = 1
    back_sine = 2 * np.sin(even)
    back_sine[0] = alternating
    back_even = np.concatenate([back_cosine, back_sine], 0).T * scale
    back_odd = np.concatenate([2 * np.cos(odd), 2 * np.sin(odd)], 0).T * scale
    index = np.arange(breadth)
    angle = index[:, None] * index[None, :] % breadth * (2 * math.pi / breadth)
    cosine, sine = np.cos(angle) / math.sqrt(breadth), np.sin(angle) / math.sqrt(breadth)
    across = np.block([[cosine, -sine], [sine, cosine]])
    pairs = [halves(t) for t in (ahead_even, ahead_odd, across, back_even, back_odd)]
    return [half_table for pair in pairs for half_table in pair]


def split(x):
    high = x.astype(BF16)
    return high, (x - high.astype(F32)).astype(BF16)


def dot(a, b):
    return jnp.dot(a, b, preferred_element_type=F32)


def table_times(high, low, x):
    x_high, x_low = split(x)
    breadth = x.shape[1]
    both = dot(high[...], jnp.concatenate([x_high, x_low], 1))
    return both[:, :breadth] + both[:, breadth:] + dot(low[...], x_high)


def times_table(x, high, low):
    x_high, x_low = split(x)
    return dot(x_high, high[...]) + (dot(x_low, high[...]) + dot(x_high, low[...]))


def rows_of(shape):
    return lax.broadcasted_iota(I32, shape, 0)


def forward(x, even, odd, across):
    height, breadth = x.shape
    half, quarter = height // 2, height // 4
    top, bottom = x[:half], x[half:]
    e = table_times(*even, top + bottom)
    o = table_times(*odd, top - bottom)
    first = rows_of((quarter, breadth)) == 0
    sine = e[quarter:]
    last = jnp.where(rows_of((PAD, breadth)) == 0, sine[:PAD], 0.0)
    mixed = jnp.concatenate(
        [
            jnp.concatenate([e[:quarter], jnp.where(first, 0.0, sine)], 1),
            jnp.concatenate([o[:quarter], o[quarter:]], 1),
            jnp.concatenate([last, jnp.zeros_like(last)], 1),
        ],
        0,
    )
    return times_table(mixed, *across)


def peak_of(fixed, moving, across, even, odd):
    breadth = fixed.shape[1] // 2
    half = fixed.shape[0] - PAD
    quarter = half // 2
    fr, fi = fixed[:, :breadth], fixed[:, breadth:]
    gr, gi = moving[:, :breadth], moving[:, breadth:]
    real = fr * gr + fi * gi
    minus = fr * gi - fi * gr
    factor = lax.rsqrt(real * real + minus * minus + FLOOR**2)
    v = times_table(jnp.concatenate([real * factor, minus * factor], 1), *across)
    vr, vn = v[:, :breadth], v[:, breadth:]
    first = rows_of((quarter, breadth)) == 0
    last = jnp.broadcast_to(vr[half : half + 1], (quarter, breadth))
    e = table_times(*even, jnp.concatenate([vr[:quarter], jnp.where(first, last, vn[:quarter])], 0))
    o = table_times(*odd, jnp.concatenate([vr[quarter:half], vn[quarter:half]], 0))
    highest = e + jnp.abs(o)
    return jnp.max(jnp.max(highest, axis=0, keepdims=True), axis=1, keepdims=True)


def weight_of(peak):
    return 1.0 / (1.0 + jnp.exp(-(peak - CENTER)))


def rolled(x, down, across):
    height, breadth = x.shape
    x = pltpu.roll(x, jnp.where(across < 0, across + breadth, across), 1)
    return pltpu.roll(x, jnp.where(down < 0, down + height, down), 0)


def choose(value, low, high, act):
    if high - low == 1:
        act(low)
        return
    middle = (low + high) // 2

    @pl.when(value < middle)
    def _():
        choose(value, low, middle, act)

    @pl.when(value >= middle)
    def _():
        choose(value, middle, high, act)


def spread_kernel(count, sizes, pieces_ref, dest_ref, slot_ref, live_ref, moving_ref, *rest):
    slab, tile, capacity = sizes
    outs, slots_ref = rest[:slab], rest[slab]
    labels, sem = rest[slab + 1 :]
    planes, height, breadth = moving_ref.shape[1:]
    run = height // slab
    here = lax.axis_index("slab")
    copies = []
    for k in reversed(range(slab)):
        rows = pl.ds(pl.multiple_of((here ^ k) * run, run), run)
        for s in range(planes):
            copy = pltpu.make_async_copy(
                moving_ref.at[0, s, rows], outs[k].at[pl.ds(s * run, run)], sem.at[k, s]
            )
            copy.start()
            copies.append(copy)
    pieces = pieces_ref[...]
    size = count
    row = jnp.broadcast_to(pieces, (size, size))
    i, j = rows_of((size, size)), lax.broadcasted_iota(I32, (size, size), 1)
    column = jnp.broadcast_to(
        jnp.sum(jnp.where(i == j, row, 0).astype(F32), axis=1, keepdims=True), (size, size)
    ).astype(I32)
    same = (lax.shift_right_arithmetic(row, 4) == lax.shift_right_arithmetic(column, 4)) & (i < j)
    rank = jnp.sum(same.astype(F32), axis=0, keepdims=True).astype(I32)
    place = lax.shift_right_arithmetic(pieces, 4) * capacity + rank
    slots_ref[...] = jnp.broadcast_to(place, slots_ref.shape)
    lane = lax.broadcasted_iota(I32, (1, size), 1)
    kept = lane < jnp.minimum(live_ref[0] * PIECES, count)
    within = jnp.where(kept, (pieces & (OWNED - 1)) + 1, 0).astype(F32)
    block = tile * capacity
    target = jnp.zeros((block, breadth), F32)
    for s in range(planes):
        value = (dest_ref[0, s] * planes + slot_ref[0, s]).astype(F32)
        target = jnp.where(rows_of((block, breadth)) == s, value, target)
    right = lax.broadcasted_iota(I32, (block, breadth), 1) >= breadth // 2
    for p in range(slab):
        match = (jnp.broadcast_to(place, (block, size)) - p * block) == rows_of((block, size))
        label = jnp.sum(jnp.where(match, within, 0.0), axis=1, keepdims=True) - 1.0
        labels[p] = jnp.where(right, target, jnp.broadcast_to(label, (block, breadth)))
    for k in range(slab):
        outs[k][pl.ds(planes * run, block), :] = labels[here ^ k]
    for copy in copies:
        copy.wait()


def pair_kernel(sizes, dest_ref, slot_ref, moving_ref, after_ref, *rest):
    tile, capacity = sizes
    outs, sem = rest[:tile], rest[tile]
    planes, height, breadth = moving_ref.shape[1:]
    here = lax.axis_index("tile")
    steps, ranks = [], []
    for s in range(planes):
        steps.append(dest_ref[1, s] ^ here)
        ranks.append(sum(((steps[u] == steps[s]).astype(I32) for u in range(s)), jnp.int32(0)))

        def act(k, s=s):
            rows = pl.ds(pl.multiple_of(ranks[s] * height, height), height)
            pltpu.make_async_copy(moving_ref.at[1, s], outs[k].at[rows], sem.at[s]).start()

        choose(steps[s], 0, tile, act)
    for k in range(tile):
        label = jnp.full((TILE, breadth), -1.0, F32)
        for s in range(planes):
            rank = jnp.where(steps[s] == k, ranks[s], TILE)
            label = jnp.where(rows_of((TILE, breadth)) == rank, slot_ref[1, s].astype(F32), label)
        outs[k][pl.ds(capacity * height, TILE), :] = label
    for s in range(planes):
        pltpu.make_async_copy(
            moving_ref.at[1, s], outs[0].at[pl.ds(0, height)], sem.at[s]
        ).wait()


def route_kernel(sizes, *rest):
    slab, planes, run, breadth = sizes
    ins, outs = rest[:slab], rest[slab : 2 * slab]
    tags, tag_sem, sem = rest[2 * slab :]
    here = lax.axis_index("slab")
    reads = [
        pltpu.make_async_copy(ins[k].at[pl.ds(planes * run, TILE)], tags.at[k], tag_sem.at[k])
        for k in range(slab)
    ]
    for read in reads:
        read.start()
    for k in range(slab):
        reads[k].wait()
        for s in range(planes):
            target = tags[k, s, breadth - 1].astype(I32)
            rows = pl.ds(pl.multiple_of((target % planes) * run, run), run)

            def act(m, k=k, s=s, rows=rows):
                source = ins[k].at[pl.ds(s * run, run)]
                pltpu.make_async_copy(source, outs[m].at[rows], sem.at[k, s]).start()

            choose((target // planes) ^ here, 0, slab, act)
    for k in range(slab):
        for s in range(planes):
            source = ins[k].at[pl.ds(s * run, run)]
            pltpu.make_async_copy(source, outs[0].at[pl.ds(0, run)], sem.at[k, s]).wait()


def label_kernel(sizes, *rest):
    slab, tile, capacity, top = sizes
    ins, outs = rest[:slab], rest[slab:]
    breadth = outs[0].shape[1]
    slab_here, tile_here = lax.axis_index("slab"), lax.axis_index("tile")
    lane = lax.broadcasted_iota(I32, (1, breadth), 1)
    for m in range(tile):
        first = top + (tile_here ^ m) * capacity
        for k in range(slab):
            line = ins[k][pl.ds(first + capacity - 1, 1), :]
            for r in reversed(range(capacity - 1)):
                line = jnp.where(lane < (r + 1) * TILE, ins[k][pl.ds(first + r, 1), :], line)
            outs[m][pl.ds(slab_here ^ k, 1), :] = line


def spectrum_kernel(live_ref, plane_ref, *rest):
    tabs, out_ref = rest[:6], rest[6]

    def body(t, _):
        out_ref[t] = forward(plane_ref[t], tabs[0:2], tabs[2:4], tabs[4:6])
        return 0

    lax.fori_loop(0, live_ref[0], body, 0)


def second_kernel(sizes, live_ref, shift_ref, plane_ref, fixed_ref, *rest):
    tile, capacity = sizes
    tabs, ins = rest[:10], rest[10 : 10 + tile]
    sum_ref, stat_ref = rest[11 + tile : 13 + tile]
    held, tags, anchor, sem, tag_sem = rest[13 + tile :]
    height, breadth = held.shape[1:]
    line = rows_of((TILE, breadth))
    reads = [
        pltpu.make_async_copy(ins[k].at[pl.ds(capacity * height, TILE)], tags.at[k], tag_sem.at[k])
        for k in range(tile)
    ]
    for read in reads:
        read.start()
    for k in range(tile):
        reads[k].wait()
        for r in range(capacity):
            label = tags[k, r, 0].astype(I32)

            @pl.when(label >= 0)
            def _(k=k, r=r, label=label):
                anchor[label] = k * capacity + r

    def fetch(t):
        def act(k):
            rows = pl.ds(pl.multiple_of(anchor[t] % capacity * height, height), height)
            pltpu.make_async_copy(ins[k].at[rows], held.at[t], sem.at[t]).start()

        choose(anchor[t] // capacity, 0, tile, act)

    for t in range(held.shape[0]):
        fetch(t)
        stat_ref[t] = jnp.zeros((TILE, breadth), F32)

    for t in range(held.shape[0]):
        pltpu.make_async_copy(ins[0].at[pl.ds(0, height)], held.at[t], sem.at[t]).wait()

    def body(t, _):
        partner = held[t]
        moving = forward(partner, tabs[0:2], tabs[2:4], tabs[4:6])
        peak = peak_of(fixed_ref[t], moving, tabs[4:6], tabs[6:8], tabs[8:10])
        weight = weight_of(peak)
        moved = rolled(partner, shift_ref[1, 0, t], shift_ref[1, 1, t])
        sum_ref[t] = plane_ref[t] + weight * moved
        stat_ref[t] = jnp.where(line == 0, jnp.broadcast_to(weight, line.shape), peak)
        return 0

    lax.fori_loop(0, live_ref[0], body, 0)


def first_kernel(slab, live_ref, shift_ref, slot_ref, sum_ref, stat_ref, fixed_ref, *rest):
    tabs, ins = rest[:10], rest[10 : 10 + slab]
    send_ref, peak_ref, plane = rest[10 + slab :]
    height, breadth = plane.shape
    run = height // slab
    band = height // PIECES
    here = lax.axis_index("slab")
    line = rows_of((TILE, breadth))
    peak_ref[...] = jnp.zeros_like(peak_ref)

    def body(t, _):
        for k in range(slab):
            rows = pl.ds(pl.multiple_of((here ^ k) * run, run), run)
            plane[rows, :] = ins[k][pl.ds(pl.multiple_of(t * run, run), run), :]
        partner = plane[...]
        moving = forward(partner, tabs[0:2], tabs[2:4], tabs[4:6])
        peak = peak_of(fixed_ref[t], moving, tabs[4:6], tabs[6:8], tabs[8:10])
        weight = weight_of(peak)
        other = stat_ref[t][0:1, 0:1]
        moved = rolled(partner, shift_ref[0, 0, t], shift_ref[0, 1, t])
        merged = (sum_ref[t] + weight * moved) / (1.0 + weight + other)
        peak_ref[t] = jnp.where(line == 0, jnp.broadcast_to(peak, line.shape), stat_ref[t])
        for b in range(PIECES):
            start = pl.multiple_of(slot_ref[0, t * PIECES + b] * band, band)
            send_ref[pl.ds(start, band), :] = merged[b * band : (b + 1) * band]
        return 0

    lax.fori_loop(0, live_ref[0], body, 0)


def gather_kernel(sizes, data_ref, *rest):
    slab, tile, capacity = sizes
    ins, out_ref = rest[:tile], rest[tile]
    tags, tag_sem = rest[tile + 1 :]
    band = out_ref.shape[1]
    tile_here = lax.axis_index("tile")
    reads = [pltpu.make_async_copy(ins[m], tags.at[m], tag_sem.at[m]) for m in range(tile)]
    for read in reads:
        read.start()
    out_ref[...] = jnp.zeros_like(out_ref)
    for read in reads:
        read.wait()

    def add(n, _):
        p, q = n // tile, n % tile
        for r in range(capacity):
            label = tags[q ^ tile_here, p, r * TILE].astype(I32)
            start = pl.multiple_of((n * capacity + r) * band, band)

            @pl.when(label >= 0)
            def _(label=label, start=start):
                out_ref[label] += data_ref[pl.ds(start, band), :]

        return 0

    lax.fori_loop(0, slab * tile, add, 0)


def call(kernel, out_shape, room=4, cost=(1_000_000, 4_000_000), **kwargs):
    return pl.pallas_call(
        kernel,
        out_shape=out_shape,
        compiler_params=pltpu.CompilerParams(vmem_limit_bytes=room << 20),
        cost_estimate=pl.CostEstimate(flops=cost[0], bytes_accessed=cost[1], transcendentals=0),
        **kwargs,
    )


def exchange(arrays, axis):
    size = len(arrays)
    got = [arrays[0]] + [None] * (size - 1)
    for k in reversed(range(1, size)):
        got[k] = lax.ppermute(arrays[k], axis, [(i, i ^ k) for i in range(size)])
    return got


def local(fixed_planes, moving_planes, pair_dest, pair_slot, plane_shift, live_count, piece_block):
    planes, height, breadth = fixed_planes.shape
    slab, tile = lax.axis_size("slab"), lax.axis_size("tile")
    devices = slab * tile
    count = piece_block.shape[0]
    run = height // slab
    band = height // PIECES
    tile_capacity = max(2, (planes + tile - 1) // tile)
    capacity = max(2, (count + devices - 1) // devices)
    block = tile * capacity
    spectrum_rows = height // 2 + PAD
    dma = pltpu.SemaphoreType.DMA
    shape = jax.ShapeDtypeStruct
    tabs = [jnp.asarray(t) for t in tables(height, breadth)]
    moving_planes, pair_dest, pair_slot, plane_shift = [
        pltpu.with_memory_space_constraint(x, pltpu.HBM)
        for x in (moving_planes, pair_dest, pair_slot, plane_shift)
    ]

    spread = call(
        functools.partial(spread_kernel, count, (slab, tile, capacity)),
        [shape((planes * run + block, breadth), F32)] * slab + [shape((TILE, count), I32)],
        in_specs=[VMEM, SMEM, SMEM, SMEM, HBM],
        out_specs=[VMEM] * (slab + 1),
        scratch_shapes=[pltpu.VMEM((slab, block, breadth), F32), dma((slab, planes))],
        name="spread",
    )(piece_block.reshape(1, count), pair_dest, pair_slot, live_count, moving_planes)
    slots = spread[slab]
    runs = exchange(spread[:slab], "slab")

    paired = call(
        functools.partial(pair_kernel, (tile, tile_capacity)),
        [shape((tile_capacity * height + TILE, breadth), F32)] * tile,
        in_specs=[SMEM, SMEM, HBM, VMEM],
        out_specs=[VMEM] * tile,
        scratch_shapes=[dma((planes,))],
        name="pair",
    )(pair_dest, pair_slot, moving_planes, slots)
    second_partners = exchange(paired, "tile")

    spectrum = call(
        spectrum_kernel,
        shape((planes, spectrum_rows, 2 * breadth), F32),
        in_specs=[SMEM] + [VMEM] * 7,
        out_specs=VMEM,
        cost=(10**9, 4 * 10**6),
        name="spectrum",
    )(live_count, fixed_planes, *tabs[:6])

    routed = call(
        functools.partial(route_kernel, (slab, planes, run, breadth)),
        [shape((planes * run, breadth), F32)] * slab,
        in_specs=[VMEM] * slab,
        out_specs=[VMEM] * slab,
        scratch_shapes=[pltpu.SMEM((slab, TILE, breadth), F32), dma((slab,)), dma((slab, planes))],
        name="route",
    )(*runs)
    first_partners = exchange(routed, "slab")

    labels = call(
        functools.partial(label_kernel, (slab, tile, capacity, planes * run)),
        [shape((slab, breadth), F32)] * tile,
        in_specs=[VMEM] * slab,
        out_specs=[VMEM] * tile,
        name="label",
    )(*runs)
    band_labels = exchange(labels, "tile")

    summed, stats = call(
        functools.partial(second_kernel, (tile, tile_capacity)),
        [shape((planes, height, breadth), F32), shape((planes, TILE, breadth), F32)],
        in_specs=[SMEM, SMEM] + [VMEM] * (12 + tile) + [VMEM],
        out_specs=[VMEM, VMEM],
        scratch_shapes=[
            pltpu.VMEM((planes, height, breadth), F32),
            pltpu.SMEM((tile, TILE, breadth), F32),
            pltpu.SMEM((planes,), I32),
            dma((planes,)),
            dma((tile,)),
        ],
        cost=(2 * 10**9, 6 * 10**6),
        room=6,
        name="second",
    )(live_count, plane_shift, fixed_planes, spectrum, *tabs, *second_partners, routed[0])

    send, tops = call(
        functools.partial(first_kernel, slab),
        [shape((devices * capacity * band, breadth), F32), shape((planes, TILE, breadth), F32)],
        in_specs=[SMEM, SMEM, SMEM] + [VMEM] * (13 + slab),
        out_specs=[VMEM, VMEM],
        scratch_shapes=[pltpu.VMEM((height, breadth), F32)],
        cost=(2 * 10**9, 6 * 10**6),
        room=8,
        name="first",
    )(live_count, plane_shift, slots, summed, stats, spectrum, *tabs, *first_partners)

    arrived = lax.all_to_all(
        send.reshape(devices, capacity * band, breadth), ("slab", "tile"), 0, 0, tiled=True
    )
    blocks = call(
        functools.partial(gather_kernel, (slab, tile, capacity)),
        shape((OWNED, band, breadth), F32),
        in_specs=[VMEM] * (tile + 1),
        out_specs=VMEM,
        scratch_shapes=[pltpu.SMEM((tile, slab, breadth), F32), dma((tile,))],
        room=8,
        name="gather",
    )(arrived.reshape(devices * capacity * band, breadth), *band_labels)
    return (jnp.transpose(tops[:, :2, 0]), blocks)


def solution(mesh):
    placed = (
        P(("slab", "tile"), None, None),
        P(None, ("slab", "tile"), None, None),
        P(None, ("slab", "tile")),
        P(None, ("slab", "tile")),
        P(None, None, ("slab", "tile")),
        P(("slab", "tile")),
        P(("slab", "tile")),
    )
    return jax.shard_map(
        local,
        mesh=mesh,
        in_specs=placed,
        out_specs=(P(None, ("slab", "tile")), P(("slab", "tile"), None, None)),
        check_vma=False,
    )
```

```python
import functools
import math

import jax
import jax.numpy as jnp
import numpy as np
from jax import lax
from jax.experimental import pallas as pl
from jax.experimental.pallas import tpu as pltpu
from jax.sharding import PartitionSpec as P

PIECES = 16
OWNED = 16
FLOOR = 0.25
CENTER = 4.0
PAD = 16
TILE = 8
F32, BF16, I32 = jnp.float32, jnp.bfloat16, jnp.int32
VMEM = pl.BlockSpec(memory_space=pltpu.VMEM)
HBM = pl.BlockSpec(memory_space=pltpu.HBM)
SMEM = pl.BlockSpec(memory_space=pltpu.SMEM)


def halves(table):
    high = np.asarray(table, np.float32).astype(jnp.bfloat16)
    low = np.asarray(table - high.astype(np.float64), np.float32).astype(jnp.bfloat16)
    return high, low


@functools.lru_cache
def tables(height, breadth):
    half, quarter = height // 2, height // 4
    rows = np.arange(half)
    even = np.arange(quarter)[:, None] * 2 * rows[None, :] % height * (2 * math.pi / height)
    odd = (np.arange(quarter)[:, None] * 2 + 1) * rows[None, :] % height * (2 * math.pi / height)
    scale = 1 / math.sqrt(height)
    alternating = np.cos(math.pi * rows)
    even_sine = -np.sin(even)
    even_sine[0] = alternating
    ahead_even = np.concatenate([np.cos(even), even_sine], 0) * scale
    ahead_odd = np.concatenate([np.cos(odd), -np.sin(odd)], 0) * scale
    back_cosine = 2 * np.cos(even)
    back_cosine[0] = 1
    back_sine = 2 * np.sin(even)
    back_sine[0] = alternating
    back_even = np.concatenate([back_cosine, back_sine], 0).T * scale
    back_odd = np.concatenate([2 * np.cos(odd), 2 * np.sin(odd)], 0).T * scale
    index = np.arange(breadth)
    angle = index[:, None] * index[None, :] % breadth * (2 * math.pi / breadth)
    cosine, sine = np.cos(angle) / math.sqrt(breadth), np.sin(angle) / math.sqrt(breadth)
    across = np.block([[cosine, -sine], [sine, cosine]])
    pairs = [halves(t) for t in (ahead_even, ahead_odd, across, back_even, back_odd)]
    return [half_table for pair in pairs for half_table in pair]


def split(x):
    high = x.astype(BF16)
    return high, (x - high.astype(F32)).astype(BF16)


def dot(a, b):
    return jnp.dot(a, b, preferred_element_type=F32)


def table_times(high, low, xs):
    parts = [split(x) for x in xs]
    breadth = xs[0].shape[1]
    shared = dot(low[...], jnp.concatenate([part[0] for part in parts], 1))
    sums = []
    for n, part in enumerate(parts):
        both = dot(high[...], jnp.concatenate(part, 1))
        sums.append(
            both[:, :breadth] + both[:, breadth:] + shared[:, n * breadth : (n + 1) * breadth]
        )
    return sums


def times_table(x, high, low):
    x_high, x_low = split(x)
    return dot(x_high, high[...]) + (dot(x_low, high[...]) + dot(x_high, low[...]))


def rows_of(shape):
    return lax.broadcasted_iota(I32, shape, 0)


def forward(xs, even, odd, across):
    height, breadth = xs[0].shape
    half, quarter = height // 2, height // 4
    first = rows_of((quarter, breadth)) == 0
    evens = table_times(*even, [x[:half] + x[half:] for x in xs])
    odds = table_times(*odd, [x[:half] - x[half:] for x in xs])
    spectra = []
    for e, o in zip(evens, odds):
        sine = e[quarter:]
        last = jnp.where(rows_of((PAD, breadth)) == 0, sine[:PAD], 0.0)
        mixed = jnp.concatenate(
            [
                jnp.concatenate([e[:quarter], jnp.where(first, 0.0, sine)], 1),
                jnp.concatenate([o[:quarter], o[quarter:]], 1),
                jnp.concatenate([last, jnp.zeros_like(last)], 1),
            ],
            0,
        )
        spectra.append(times_table(mixed, *across))
    return spectra


def peaks_of(fixed, moving, across, even, odd):
    breadth = fixed[0].shape[1] // 2
    half = fixed[0].shape[0] - PAD
    quarter = half // 2
    first = rows_of((quarter, breadth)) == 0
    lower, upper = [], []
    for f, g in zip(fixed, moving):
        fr, fi = f[:, :breadth], f[:, breadth:]
        gr, gi = g[:, :breadth], g[:, breadth:]
        real = fr * gr + fi * gi
        minus = fr * gi - fi * gr
        factor = lax.rsqrt(real * real + minus * minus + FLOOR**2)
        v = times_table(jnp.concatenate([real * factor, minus * factor], 1), *across)
        vr, vn = v[:, :breadth], v[:, breadth:]
        last = jnp.broadcast_to(vr[half : half + 1], (quarter, breadth))
        lower.append(jnp.concatenate([vr[:quarter], jnp.where(first, last, vn[:quarter])], 0))
        upper.append(jnp.concatenate([vr[quarter:half], vn[quarter:half]], 0))
    peaks = []
    for e, o in zip(table_times(*even, lower), table_times(*odd, upper)):
        highest = jnp.max(e + jnp.abs(o), axis=0, keepdims=True)
        peaks.append(jnp.max(highest, axis=1, keepdims=True))
    return peaks


def weight_of(peak):
    return 1.0 / (1.0 + jnp.exp(-(peak - CENTER)))


def rolled(x, down, across):
    height, breadth = x.shape
    x = pltpu.roll(x, jnp.where(across < 0, across + breadth, across), 1)
    return pltpu.roll(x, jnp.where(down < 0, down + height, down), 0)


def choose(value, low, high, act):
    if high - low == 1:
        act(low)
        return
    middle = (low + high) // 2

    @pl.when(value < middle)
    def _():
        choose(value, low, middle, act)

    @pl.when(value >= middle)
    def _():
        choose(value, middle, high, act)


def spread_kernel(count, sizes, pieces_hbm, dest_hbm, slot_hbm, live_hbm, moving_ref, *rest):
    slab, tile, capacity = sizes
    outs, slots_ref, live_out = rest[:slab], rest[slab], rest[slab + 1]
    pieces_ref, dest_ref, slot_ref, live_ref, labels, small_sem, sem = rest[slab + 2 :]
    planes, height, breadth = moving_ref.shape[1:]
    run = height // slab
    here = lax.axis_index("slab")
    small = [
        pltpu.make_async_copy(source, target, small_sem.at[n])
        for n, (source, target) in enumerate(
            (
                (pieces_hbm, pieces_ref),
                (dest_hbm, dest_ref),
                (slot_hbm, slot_ref),
                (live_hbm, live_ref),
            )
        )
    ]
    for copy in small:
        copy.start()
    copies = []
    for k in reversed(range(slab)):
        rows = pl.ds(pl.multiple_of((here ^ k) * run, run), run)
        copy = pltpu.make_async_copy(
            moving_ref.at[0, :, rows, :],
            outs[k].at[pl.ds(0, planes * run)].reshape(planes, run, breadth),
            sem.at[k],
        )
        copy.start()
        copies.append(copy)
    for copy in small:
        copy.wait()
    live_out[0] = live_ref[0, 0]
    pieces = pieces_ref[...]
    size = count
    row = jnp.broadcast_to(pieces, (size, size))
    i, j = rows_of((size, size)), lax.broadcasted_iota(I32, (size, size), 1)
    column = jnp.broadcast_to(
        jnp.sum(jnp.where(i == j, row, 0).astype(F32), axis=1, keepdims=True), (size, size)
    ).astype(I32)
    same = (lax.shift_right_arithmetic(row, 4) == lax.shift_right_arithmetic(column, 4)) & (i < j)
    rank = jnp.sum(same.astype(F32), axis=0, keepdims=True).astype(I32)
    place = lax.shift_right_arithmetic(pieces, 4) * capacity + rank
    slots_ref[...] = jnp.broadcast_to(place, slots_ref.shape)
    lane = lax.broadcasted_iota(I32, (1, size), 1)
    kept = lane < jnp.minimum(live_ref[0, 0] * PIECES, count)
    within = jnp.where(kept, (pieces & (OWNED - 1)) + 1, 0).astype(F32)
    block = tile * capacity
    target = jnp.zeros((block, breadth), F32)
    for s in range(planes):
        value = (dest_ref[0, s] * planes + slot_ref[0, s]).astype(F32)
        target = jnp.where(rows_of((block, breadth)) == s, value, target)
    right = lax.broadcasted_iota(I32, (block, breadth), 1) >= breadth // 2
    for p in range(slab):
        match = (jnp.broadcast_to(place, (block, size)) - p * block) == rows_of((block, size))
        label = jnp.sum(jnp.where(match, within, 0.0), axis=1, keepdims=True) - 1.0
        labels[p] = jnp.where(right, target, jnp.broadcast_to(label, (block, breadth)))
    for k in range(slab):
        outs[k][pl.ds(planes * run, block), :] = labels[here ^ k]
    for copy in copies:
        copy.wait()


def pair_kernel(sizes, dest_ref, slot_ref, moving_ref, after_ref, *rest):
    tile, capacity = sizes
    outs, sem = rest[:tile], rest[tile]
    planes, height, breadth = moving_ref.shape[1:]
    here = lax.axis_index("tile")
    steps, ranks = [], []
    for s in range(planes):
        steps.append(dest_ref[1, s] ^ here)
        ranks.append(sum(((steps[u] == steps[s]).astype(I32) for u in range(s)), jnp.int32(0)))

        def act(k, s=s):
            rows = pl.ds(pl.multiple_of(ranks[s] * height, height), height)
            pltpu.make_async_copy(moving_ref.at[1, s], outs[k].at[rows], sem.at[s]).start()

        choose(steps[s], 0, tile, act)
    for k in range(tile):
        label = jnp.full((TILE, breadth), -1.0, F32)
        for s in range(planes):
            rank = jnp.where(steps[s] == k, ranks[s], TILE)
            label = jnp.where(rows_of((TILE, breadth)) == rank, slot_ref[1, s].astype(F32), label)
        outs[k][pl.ds(capacity * height, TILE), :] = label
    for s in range(planes):
        pltpu.make_async_copy(
            moving_ref.at[1, s], outs[0].at[pl.ds(0, height)], sem.at[s]
        ).wait()


def route_kernel(sizes, *rest):
    slab, first, last, planes, run, breadth = sizes
    ins, outs = rest[: last - first], rest[-slab - 2 : -2]
    tags, tag_sem = rest[-2:]
    here = lax.axis_index("slab")
    reads = [
        pltpu.make_async_copy(ref.at[pl.ds(planes * run, TILE)], tags.at[k], tag_sem.at[k])
        for k, ref in enumerate(ins)
    ]
    for read in reads:
        read.start()
    for read in reads:
        read.wait()
    for k, ref in enumerate(ins):

        def move(s, _, k=k, ref=ref):
            target = tags[k, s, breadth - 1].astype(I32)
            rows = pl.ds(pl.multiple_of((target % planes) * run, run), run)

            def act(m):
                outs[m][rows, :] = ref[pl.ds(pl.multiple_of(s * run, run), run), :]

            choose((target // planes) ^ here, 0, slab, act)
            return 0

        lax.fori_loop(0, planes, move, 0)


def label_kernel(sizes, *rest):
    slab, tile, capacity, top = sizes
    ins, outs = rest[:slab], rest[slab:]
    breadth = outs[0].shape[1]
    slab_here, tile_here = lax.axis_index("slab"), lax.axis_index("tile")
    lane = lax.broadcasted_iota(I32, (1, breadth), 1)
    for m in range(tile):
        first = top + (tile_here ^ m) * capacity
        for k in range(slab):
            line = ins[k][pl.ds(first + capacity - 1, 1), :]
            for r in reversed(range(capacity - 1)):
                line = jnp.where(lane < (r + 1) * TILE, ins[k][pl.ds(first + r, 1), :], line)
            outs[m][pl.ds(slab_here ^ k, 1), :] = line


def spectrum_kernel(live_ref, plane_ref, *rest):
    tabs, out_ref = rest[:6], rest[6]
    group = group_of(plane_ref.shape[0])

    def body(i, _):
        xs = [plane_ref[i * group + n] for n in range(group)]
        for n, y in enumerate(forward(xs, tabs[0:2], tabs[2:4], tabs[4:6])):
            out_ref[i * group + n] = y
        return 0

    lax.fori_loop(0, (live_ref[0] + group - 1) // group, body, 0)


def second_kernel(sizes, live_ref, shift_ref, plane_ref, fixed_ref, *rest):
    tile, capacity = sizes
    tabs, ins = rest[:10], rest[10 : 10 + tile]
    sum_ref, stat_ref = rest[11 + tile : 13 + tile]
    held, tags, anchor, sem, tag_sem = rest[13 + tile :]
    height, breadth = held.shape[1:]
    line = rows_of((TILE, breadth))
    reads = [
        pltpu.make_async_copy(ins[k].at[pl.ds(capacity * height, TILE)], tags.at[k], tag_sem.at[k])
        for k in range(tile)
    ]
    for read in reads:
        read.start()
    for k in range(tile):
        reads[k].wait()
        for r in range(capacity):
            label = tags[k, r, 0].astype(I32)

            @pl.when(label >= 0)
            def _(k=k, r=r, label=label):
                anchor[label] = k * capacity + r

    def fetch(t):
        def act(k):
            rows = pl.ds(pl.multiple_of(anchor[t] % capacity * height, height), height)
            pltpu.make_async_copy(ins[k].at[rows], held.at[t], sem.at[t]).start()

        choose(anchor[t] // capacity, 0, tile, act)

    for t in range(held.shape[0]):
        fetch(t)
        stat_ref[t] = jnp.zeros((TILE, breadth), F32)

    for t in range(held.shape[0]):
        pltpu.make_async_copy(ins[0].at[pl.ds(0, height)], held.at[t], sem.at[t]).wait()

    group = group_of(held.shape[0])

    def body(i, _):
        ts = [i * group + n for n in range(group)]
        partners = [held[t] for t in ts]
        moving = forward(partners, tabs[0:2], tabs[2:4], tabs[4:6])
        fixed = [fixed_ref[t] for t in ts]
        peaks = peaks_of(fixed, moving, tabs[4:6], tabs[6:8], tabs[8:10])
        for t, peak in zip(ts, peaks):

            @pl.when(t < live_ref[0])
            def _(t=t, peak=peak):
                weight = weight_of(peak)
                moved = rolled(held[t], shift_ref[1, 0, t], shift_ref[1, 1, t])
                sum_ref[t] = plane_ref[t] + weight * moved
                stat_ref[t] = jnp.where(line == 0, jnp.broadcast_to(weight, line.shape), peak)

        return 0

    lax.fori_loop(0, (live_ref[0] + group - 1) // group, body, 0)


def first_kernel(slab, live_ref, shift_hbm, slot_vmem, sum_ref, stat_ref, fixed_ref, *rest):
    tabs, ins = rest[:10], rest[10 : 10 + slab]
    send_ref, peak_ref, plane, shift_ref, slot_ref, sem = rest[10 + slab :]
    group, height, breadth = plane.shape
    run = height // slab
    band = height // PIECES
    here = lax.axis_index("slab")
    line = rows_of((TILE, breadth))
    small = [
        pltpu.make_async_copy(shift_hbm, shift_ref, sem.at[0]),
        pltpu.make_async_copy(slot_vmem, slot_ref, sem.at[1]),
    ]
    for copy in small:
        copy.start()
    peak_ref[...] = jnp.zeros_like(peak_ref)

    def body(i, _):
        ts = [i * group + n for n in range(group)]
        for n, t in enumerate(ts):
            for k in range(slab):
                rows = pl.ds(pl.multiple_of((here ^ k) * run, run), run)
                plane[n, rows, :] = ins[k][pl.ds(pl.multiple_of(t * run, run), run), :]
        moving = forward([plane[n] for n in range(group)], tabs[0:2], tabs[2:4], tabs[4:6])
        fixed = [fixed_ref[t] for t in ts]
        peaks = peaks_of(fixed, moving, tabs[4:6], tabs[6:8], tabs[8:10])

        @pl.when(i == 0)
        def _():
            for copy in small:
                copy.wait()

        for n, t in enumerate(ts):

            @pl.when(t < live_ref[0])
            def _(n=n, t=t):
                weight = weight_of(peaks[n])
                other = stat_ref[t][0:1, 0:1]
                moved = rolled(plane[n], shift_ref[0, 0, t], shift_ref[0, 1, t])
                merged = (sum_ref[t] + weight * moved) / (1.0 + weight + other)
                top = jnp.broadcast_to(peaks[n], line.shape)
                peak_ref[t] = jnp.where(line == 0, top, stat_ref[t])
                for b in range(PIECES):
                    start = pl.multiple_of(slot_ref[0, t * PIECES + b] * band, band)
                    send_ref[pl.ds(start, band), :] = merged[b * band : (b + 1) * band]

        return 0

    lax.fori_loop(0, (live_ref[0] + group - 1) // group, body, 0)


def gather_kernel(sizes, data_ref, *rest):
    slab, tile, capacity = sizes
    ins, out_ref = rest[:tile], rest[tile]
    total, tags, tag_sem = rest[tile + 1 :]
    band = out_ref.shape[1]
    tile_here = lax.axis_index("tile")
    reads = [pltpu.make_async_copy(ins[m], tags.at[m], tag_sem.at[m]) for m in range(tile)]
    for read in reads:
        read.start()
    total[...] = jnp.zeros_like(total)
    for read in reads:
        read.wait()

    def add(p, _):
        for q in range(tile):
            for r in range(capacity):
                label = tags[tile_here ^ q, p, r * TILE].astype(I32)
                target = jnp.where(label < 0, OWNED, label)
                start = pl.multiple_of(((p * tile + q) * capacity + r) * band, band)
                total[target] += data_ref[pl.ds(start, band), :]
        return 0

    lax.fori_loop(0, slab, add, 0)
    out_ref[...] = total[:OWNED]


def group_of(planes):
    return 2 if planes % 2 == 0 else 1


def call(kernel, out_shape, room=4, cost=(1_000_000, 4_000_000), **kwargs):
    return pl.pallas_call(
        kernel,
        out_shape=out_shape,
        compiler_params=pltpu.CompilerParams(vmem_limit_bytes=room << 20),
        cost_estimate=pl.CostEstimate(flops=cost[0], bytes_accessed=cost[1], transcendentals=0),
        **kwargs,
    )


def exchange(arrays, axis):
    size = len(arrays)
    got = [arrays[0]] + [None] * (size - 1)
    for k in reversed(range(1, size)):
        got[k] = lax.ppermute(arrays[k], axis, [(i, i ^ k) for i in range(size)])
    return got


def local(fixed_planes, moving_planes, pair_dest, pair_slot, plane_shift, live_count, piece_block):
    planes, height, breadth = fixed_planes.shape
    slab, tile = lax.axis_size("slab"), lax.axis_size("tile")
    devices = slab * tile
    count = piece_block.shape[0]
    run = height // slab
    band = height // PIECES
    tile_capacity = max(2, (planes + tile - 1) // tile)
    capacity = max(2, (count + devices - 1) // devices)
    block = tile * capacity
    spectrum_rows = height // 2 + PAD
    dma = pltpu.SemaphoreType.DMA
    shape = jax.ShapeDtypeStruct
    tabs = [jnp.asarray(t) for t in tables(height, breadth)]
    moving_planes, pair_dest, pair_slot, plane_shift = [
        pltpu.with_memory_space_constraint(x, pltpu.HBM)
        for x in (moving_planes, pair_dest, pair_slot, plane_shift)
    ]
    pieces = pltpu.with_memory_space_constraint(piece_block.reshape(1, count), pltpu.HBM)
    live_far = live_count.reshape(1, 1)

    spread = call(
        functools.partial(spread_kernel, count, (slab, tile, capacity)),
        [shape((planes * run + block, breadth), F32)] * slab
        + [shape((TILE, count), I32), shape((1,), I32)],
        in_specs=[HBM] * 3 + [pl.BlockSpec(memory_space=pl.ANY), HBM],
        out_specs=[VMEM] * (slab + 1) + [SMEM],
        scratch_shapes=[
            pltpu.VMEM((1, count), I32),
            pltpu.SMEM(pair_dest.shape, I32),
            pltpu.SMEM(pair_slot.shape, I32),
            pltpu.SMEM((1, 1), I32),
            pltpu.VMEM((slab, block, breadth), F32),
            dma((4,)),
            dma((slab,)),
        ],
        name="spread",
    )(pieces, pair_dest, pair_slot, live_far, moving_planes)
    slots, live_count = spread[slab:]
    runs = exchange(spread[:slab], "slab")

    paired = call(
        functools.partial(pair_kernel, (tile, tile_capacity)),
        [shape((tile_capacity * height + TILE, breadth), F32)] * tile,
        in_specs=[SMEM, SMEM, HBM, VMEM],
        out_specs=[VMEM] * tile,
        scratch_shapes=[dma((planes,))],
        name="pair",
    )(pair_dest, pair_slot, moving_planes, slots)
    second_partners = exchange(paired, "tile")

    spectrum = call(
        spectrum_kernel,
        shape((planes, spectrum_rows, 2 * breadth), F32),
        in_specs=[SMEM] + [VMEM] * 7,
        out_specs=VMEM,
        cost=(10**9, 4 * 10**6),
        name="spectrum",
    )(live_count, fixed_planes, *tabs[:6])

    routed = []
    for name, first, last in (("near", 0, slab // 2), ("far", slab // 2, slab)):
        routed = call(
            functools.partial(route_kernel, (slab, first, last, planes, run, breadth)),
            [shape((planes * run, breadth), F32)] * slab,
            in_specs=[VMEM] * (last - first + len(routed)),
            out_specs=[VMEM] * slab,
            scratch_shapes=[pltpu.SMEM((last - first, TILE, breadth), F32), dma((last - first,))],
            input_output_aliases={last - first + k: k for k in range(len(routed))},
            name=name,
        )(*runs[first:last], *routed)
    first_partners = exchange(routed, "slab")

    labels = call(
        functools.partial(label_kernel, (slab, tile, capacity, planes * run)),
        [shape((slab, breadth), F32)] * tile,
        in_specs=[VMEM] * slab,
        out_specs=[VMEM] * tile,
        name="label",
    )(*runs)
    band_labels = exchange(labels, "tile")

    summed, stats = call(
        functools.partial(second_kernel, (tile, tile_capacity)),
        [shape((planes, height, breadth), F32), shape((planes, TILE, breadth), F32)],
        in_specs=[SMEM, SMEM] + [VMEM] * (12 + tile) + [VMEM],
        out_specs=[VMEM, VMEM],
        scratch_shapes=[
            pltpu.VMEM((planes, height, breadth), F32),
            pltpu.SMEM((tile, TILE, breadth), F32),
            pltpu.SMEM((planes,), I32),
            dma((planes,)),
            dma((tile,)),
        ],
        cost=(2 * 10**9, 6 * 10**6),
        room=6,
        name="second",
    )(live_count, plane_shift, fixed_planes, spectrum, *tabs, *second_partners, routed[0])

    send, tops = call(
        functools.partial(first_kernel, slab),
        [shape((devices * capacity * band, breadth), F32), shape((planes, TILE, breadth), F32)],
        in_specs=[SMEM, HBM] + [VMEM] * (14 + slab),
        out_specs=[VMEM, VMEM],
        scratch_shapes=[
            pltpu.VMEM((group_of(planes), height, breadth), F32),
            pltpu.SMEM(plane_shift.shape, I32),
            pltpu.SMEM((TILE, count), I32),
            dma((2,)),
        ],
        cost=(2 * 10**9, 6 * 10**6),
        room=8,
        name="first",
    )(live_count, plane_shift, slots, summed, stats, spectrum, *tabs, *first_partners)

    arrived = lax.all_to_all(
        send.reshape(devices, capacity * band, breadth), ("slab", "tile"), 0, 0, tiled=True
    )
    blocks = call(
        functools.partial(gather_kernel, (slab, tile, capacity)),
        shape((OWNED, band, breadth), F32),
        in_specs=[VMEM] * (tile + 1),
        out_specs=VMEM,
        scratch_shapes=[
            pltpu.VMEM((OWNED + 1, band, breadth), F32),
            pltpu.SMEM((tile, slab, breadth), F32),
            dma((tile,)),
        ],
        room=8,
        name="gather",
    )(arrived.reshape(devices * capacity * band, breadth), *band_labels)
    return (jnp.transpose(tops[:, :2, 0]), blocks)


def solution(mesh):
    placed = (
        P(("slab", "tile"), None, None),
        P(None, ("slab", "tile"), None, None),
        P(None, ("slab", "tile")),
        P(None, ("slab", "tile")),
        P(None, None, ("slab", "tile")),
        P(("slab", "tile")),
        P(("slab", "tile")),
    )
    return jax.shard_map(
        local,
        mesh=mesh,
        in_specs=placed,
        out_specs=(P(None, ("slab", "tile")), P(("slab", "tile"), None, None)),
        check_vma=False,
    )
```
